1024 devices in a mesh: section: 32 (over y, x_hi), row: 2 (over core), col: 16 (over z, x_lo).
Axes of the slice: x: 8 (x_hi: 4, x_lo: 2; x = x_hi * 2 + x_lo), y: 8, z: 8, core: 2. Of those that a mesh axis runs over, the one named last changes fastest.
Arguments:
- inputs: bfloat16 [32, 128, 4096], P('section', 'col', 'row'), may hold values from -6 to 6
- gate_pre: bfloat16 [32, 128, 14336], P('section', None, 'col'), may hold values from -8 to 8
- up_weight: bfloat16 [4096, 14336], P('row', 'col'), may hold values from -0.09375 to 0.09375
- down_weight: bfloat16 [14336, 4096], P('col', 'row'), may hold values from -0.046875 to 0.046875
- output_grad: bfloat16 [32, 128, 4096], P('section', 'col', 'row'), may hold values from -6 to 6
Outputs:
- handed_forward: bfloat16 [32, 128, 4096], P('section', 'col', 'row')
- gate_grad: bfloat16 [32, 128, 14336], P('section', 'row', 'col')
- handed_back: bfloat16 [32, 128, 4096], P('section', 'col', 'row')
The draws below stay inside these ranges and needn't reach their ends.
All inputs are finite; a program needn't handle non-finite values.
Results may differ from the reference program's by a relative error of at most 0.0041.
Values may be sent and summed in bfloat16 or wider, within the bound.
A program may use at most 32 MiB of HBM per device.

```python
import jax
import jax.numpy as jnp

D = 4096
FF = 14336
TOK = 128
SECTIONS = 32


def level_of(key, extent, cuts, least, high):
    gain = 1.0
    for position, parts in cuts:
        heights = jax.random.uniform(jax.random.fold_in(jax.random.fold_in(key, 6), position), (parts,), jnp.float32, least / len(cuts), high / len(cuts))
        gain = gain * jnp.repeat(jnp.exp(heights), extent[position] // parts).reshape((-1,) + (1,) * (len(extent) - 1 - position))
    return gain


def gaussian(stream_key, shape, scale, reach, split=(), held_as=jnp.bfloat16):
    values = scale * jax.random.normal(stream_key, shape, jnp.float32)
    if split:
        values = values * level_of(stream_key, shape, split, -0.22, 0.18)
    return jnp.clip(values, -reach, reach).astype(held_as)


def setup_inputs(seed: int = 0) -> dict:
    key_list = jax.random.split(jax.random.key(seed), 6)
    inputs = gaussian(key_list[0], (SECTIONS, TOK, D), 1.0, 6.0, ((0, 32), (1, 16), (2, 2)))
    gate_pre = gaussian(key_list[1], (SECTIONS, TOK, FF), 1.5, 8.0, ((0, 32), (2, 16)))
    up_weight = gaussian(key_list[2], (D, FF), D ** -0.5, 0.09375, ((0, 2), (1, 16)))
    down_weight = gaussian(key_list[3], (FF, D), FF ** -0.5, 0.046875, ((0, 16), (1, 2)))
    output_grad = gaussian(key_list[4], (SECTIONS, TOK, D), 1.0, 6.0, ((0, 32), (1, 16), (2, 2)))
    return dict(inputs=inputs, gate_pre=gate_pre, up_weight=up_weight, down_weight=down_weight, output_grad=output_grad)


def reference(inputs, gate_pre, up_weight, down_weight, output_grad):
    replicas, tokens, width = inputs.shape
    flat_in = inputs.reshape(replicas * tokens, width)
    flat_grad = output_grad.reshape(replicas * tokens, width)
    gate_full = gate_pre.reshape(replicas * tokens, -1).astype(jnp.float32)
    up_act = jnp.dot(flat_in, up_weight, preferred_element_type=jnp.float32)
    sigmoid_gate = jax.nn.sigmoid(gate_full)
    hidden = (gate_full * sigmoid_gate * up_act).astype(jnp.bfloat16)
    mixed = jnp.dot(hidden, down_weight, preferred_element_type=jnp.float32)
    layer_out = (flat_in.astype(jnp.float32) + mixed).astype(jnp.bfloat16)
    hidden_grad = jnp.dot(flat_grad, down_weight.T, preferred_element_type=jnp.float32)
    up_grad = (hidden_grad * gate_full * sigmoid_gate).astype(jnp.bfloat16)
    gate_grad = (hidden_grad * up_act * sigmoid_gate * (1.0 + gate_full * (1.0 - sigmoid_gate))).astype(jnp.bfloat16)
    back_sum = jnp.dot(up_grad, up_weight.T, preferred_element_type=jnp.float32)
    input_grad = (flat_grad.astype(jnp.float32) + back_sum).astype(jnp.bfloat16)
    layer_out = layer_out.reshape(replicas, tokens, width)
    input_grad = input_grad.reshape(replicas, tokens, width)
    handed_forward = jnp.roll(layer_out, 1, axis=0)
    handed_back = jnp.roll(input_grad, -1, axis=0)
    return handed_forward, gate_grad.reshape(replicas, tokens, -1), handed_back
```

```python
import functools

import jax
import jax.numpy as jnp
from jax import lax
from jax.experimental import pallas as pl
from jax.experimental.pallas import tpu as pltpu
from jax.sharding import PartitionSpec as P

MESH = pl.DeviceIdType.MESH
F32 = jnp.float32
BF16 = jnp.bfloat16
NT = (((1,), (1,)), ((), ()))
NN = (((1,), (0,)), ((), ()))


def kernel(
    in_f, gate_in, up_in, dn_in, in_b,
    out_f, out_g, out_b,
    gf, gb, upv, dnv, gv, gs, dg,
    uf, hb, s1f, r1f, s1b, r1b, gg,
    pf, pb, sxf, rxf, sfp, rfp, sfm, rfm, sbp, rbp, sbm, rbm, sxb, rxb, hf, hbk,
    lsem, fzp_s, fzp_r, fzm_s, fzm_r, fx_s, fx_r, bzp_s, bzp_r, bzm_s, bzm_r, bx_s, bx_r,
    e_s, e_r, ffx_s, ffx_r, rfp_s, rfp_r, rfm_s, rfm_r, rbp_s, rbp_r, rbm_s, rbm_r, rx_s, rx_r, ho_s, ho_r,
):
    s = lax.axis_index("section")
    r = lax.axis_index("row")
    c = lax.axis_index("col")
    z, xl = c // 2, c % 2
    xo = 1 - xl
    ns = lax.axis_size("section")
    zp = {"col": ((z + 1) % 8) * 2 + xl}
    zm = {"col": ((z + 7) % 8) * 2 + xl}
    xp = {"col": z * 2 + xo}
    mate = {"row": 1 - r}
    nxt = {"section": (s + 1) % ns}
    prv = {"section": (s + ns - 1) % ns}

    local = []

    def fetch(src, dst, i):
        cp = pltpu.make_async_copy(src, dst, lsem.at[i])
        cp.start()
        return cp

    cp_gate = fetch(gate_in.at[0], gv, 0)
    cp_f = fetch(in_f.at[0], gf.at[z, xl], 1)
    cp_b = fetch(in_b.at[0], gb.at[z, xl], 2)
    cp_up = fetch(up_in, upv, 3)
    cp_dn = fetch(dn_in, dnv, 4)

    barrier = pltpu.get_barrier_semaphore()
    for dev in (zp, zm, xp, mate, nxt, prv):
        pl.semaphore_signal(barrier, inc=1, device_id=dev, device_id_type=MESH)
    pl.semaphore_wait(barrier, 6)

    sent = []

    def put(src, dst, ss, rs, dev):
        cp = pltpu.make_async_remote_copy(
            src_ref=src, dst_ref=dst, send_sem=ss, recv_sem=rs, device_id=dev, device_id_type=MESH
        )
        cp.start()
        sent.append(cp)

    def got(dst, rs):
        pltpu.make_async_remote_copy(
            src_ref=dst, dst_ref=dst, send_sem=rs, recv_sem=rs, device_id=zp, device_id_type=MESH
        ).wait_recv()

    put(in_f.at[0], gf.at[z, xl], fzp_s.at[0], fzp_r.at[0], zp)
    put(in_f.at[0], gf.at[z, xl], fzm_s.at[0], fzm_r.at[0], zm)
    put(in_b.at[0], gb.at[z, xl], bx_s.at[0], bx_r.at[0], xp)
    put(in_b.at[0], gb.at[z, xl], bzp_s.at[0], bzp_r.at[0], zp)
    put(in_b.at[0], gb.at[z, xl], bzm_s.at[0], bzm_r.at[0], zm)
    put(in_f.at[0], gf.at[z, xl], fx_s.at[0], fx_r.at[0], xp)

    cp_gate.wait()
    g32 = gv[...].astype(F32)
    sg = 1.0 / (1.0 + jnp.exp(-g32))
    gs[...] = g32 * sg
    dg[...] = sg * (1.0 + g32 * (1.0 - sg))

    for d in range(1, 5):
        lo, hi = (z + 8 - d) % 8, (z + d) % 8
        got(gf.at[lo, xl], fzp_r.at[d - 1])
        if d < 4:
            put(gf.at[lo, xl], gf.at[lo, xl], fzp_s.at[d], fzp_r.at[d], zp)
        put(gf.at[lo, xl], gf.at[lo, xl], fx_s.at[d], fx_r.at[d], xp)
        if d <= 3:
            got(gf.at[hi, xl], fzm_r.at[d - 1])
            if d < 3:
                put(gf.at[hi, xl], gf.at[hi, xl], fzm_s.at[d], fzm_r.at[d], zm)
            put(gf.at[hi, xl], gf.at[hi, xl], fx_s.at[4 + d], fx_r.at[4 + d], xp)
        if d == 1:
            got(gb.at[z, xo], bx_r.at[0])
            put(gb.at[z, xo], gb.at[z, xo], bzp_s.at[3], bzp_r.at[3], zp)
            put(gb.at[z, xo], gb.at[z, xo], bzm_s.at[4], bzm_r.at[4], zm)
        for half, x in ((0, xl), (1, xo)):
            if d <= 3:
                i = half * 3 + d - 1
                got(gb.at[lo, x], bzp_r.at[i])
                if d < 3:
                    put(gb.at[lo, x], gb.at[lo, x], bzp_s.at[i + 1], bzp_r.at[i + 1], zp)
            i = half * 4 + d - 1
            got(gb.at[hi, x], bzm_r.at[i])
            if d < 4:
                put(gb.at[hi, x], gb.at[hi, x], bzm_s.at[i + 1], bzm_r.at[i + 1], zm)
    got(gf.at[z, xo], fx_r.at[0])
    for d in range(1, 5):
        got(gf.at[(z + 8 - d) % 8, xo], fx_r.at[d])
        if d <= 3:
            got(gf.at[(z + d) % 8, xo], fx_r.at[4 + d])
    cp_f.wait()
    cp_b.wait()
    cp_up.wait()
    cp_dn.wait()

    cuts = ((0, 512), (512, 384))
    act = gf[...].reshape(128, 2048)
    for i, (a, w) in enumerate(cuts):
        v = lax.dot_general(act, upv[:, a : a + w], NN, preferred_element_type=F32)
        uf[:, a : a + w] = v
        s1f[:, a : a + w] = v.astype(BF16)
        put(s1f.at[:, a : a + w], r1f.at[:, a : a + w], e_s.at[i], e_r.at[i], mate)
    grd = gb[...].reshape(128, 2048)
    for i, (a, w) in enumerate(cuts):
        v = lax.dot_general(grd, dnv[a : a + w, :], NT, preferred_element_type=F32)
        hb[:, a : a + w] = v
        s1b[:, a : a + w] = v.astype(BF16)
        put(s1b.at[:, a : a + w], r1b.at[:, a : a + w], e_s.at[2 + i], e_r.at[2 + i], mate)

    for i, (a, w) in enumerate(cuts):
        got(r1f.at[:, a : a + w], e_r.at[i])
    u = uf[...] + r1f[...].astype(F32)
    uf[...] = u
    hid = (gs[...] * u).astype(BF16)
    for a in range(0, 2048, 512):
        v = lax.dot_general(hid, dnv[:, a : a + 512], NN, preferred_element_type=F32)
        pf[:, :, :, a : a + 512] = v.reshape(8, 2, 8, 512)
    order = (4, 3, -3, 2, -2, 1, -1, 0)
    for i, d in enumerate(order):
        sxf[i] = pf[(z + d + 8) % 8, xo].astype(BF16)
        put(sxf.at[i], rxf.at[i], ffx_s.at[i], ffx_r.at[i], xp)

    for i, (a, w) in enumerate(cuts):
        got(r1b.at[:, a : a + w], e_r.at[2 + i])
    h = hb[...] + r1b[...].astype(F32)
    hb[...] = h
    upg = (gs[...] * h).astype(BF16)
    for a in range(0, 2048, 512):
        v = lax.dot_general(upg, upv[a : a + 512, :], NT, preferred_element_type=F32)
        pb[:, :, :, a : a + 512] = v.reshape(8, 2, 8, 512)

    def own_f(d):
        i = order.index(d)
        got(rxf.at[i], ffx_r.at[i])
        return pf[(z + d + 8) % 8, xl] + rxf[i].astype(F32)

    for k in range(4):
        if k == 0:
            sbm[0] = pb[(z + 4) % 8].astype(BF16)
            put(sbm.at[0], rbm.at[0], rbm_s.at[0], rbm_r.at[0], zm)
            sbp[0] = pb[(z + 3) % 8].astype(BF16)
            put(sbp.at[0], rbp.at[0], rbp_s.at[0], rbp_r.at[0], zp)
            sfp[0] = own_f(4).astype(BF16)
            put(sfp.at[0], rfp.at[0], rfp_s.at[0], rfp_r.at[0], zp)
            sfm[0] = own_f(-3).astype(BF16)
            put(sfm.at[0], rfm.at[0], rfm_s.at[0], rfm_r.at[0], zm)
            rows = pl.ds(pl.multiple_of(r * 64, 64), 64)
            gg[...] = (hb[rows, :] * uf[rows, :] * dg[rows, :]).astype(BF16)
            cp_g = fetch(gg, out_g.at[0], 0)
        else:
            got(rbm.at[k - 1], rbm_r.at[k - 1])
            sbm[k] = (pb[(z + 4 + k) % 8] + rbm[k - 1].astype(F32)).astype(BF16)
            put(sbm.at[k], rbm.at[k], rbm_s.at[k], rbm_r.at[k], zm)
            if k < 3:
                got(rbp.at[k - 1], rbp_r.at[k - 1])
                sbp[k] = (pb[(z + 3 - k) % 8] + rbp[k - 1].astype(F32)).astype(BF16)
                put(sbp.at[k], rbp.at[k], rbp_s.at[k], rbp_r.at[k], zp)
            v = own_f(4 - k)
            got(rfp.at[k - 1], rfp_r.at[k - 1])
            sfp[k] = (v + rfp[k - 1].astype(F32)).astype(BF16)
            put(sfp.at[k], rfp.at[k], rfp_s.at[k], rfp_r.at[k], zp)
            if k < 3:
                v = own_f(k - 3)
                got(rfm.at[k - 1], rfm_r.at[k - 1])
                sfm[k] = (v + rfm[k - 1].astype(F32)).astype(BF16)
                put(sfm.at[k], rfm.at[k], rfm_s.at[k], rfm_r.at[k], zm)

    got(rbp.at[2], rbp_r.at[2])
    got(rbm.at[3], rbm_r.at[3])
    sxb[...] = (pb[z, xo] + rbp[2, xo].astype(F32) + rbm[3, xo].astype(F32)).astype(BF16)
    put(sxb, rxb, rx_s.at[0], rx_r.at[0], xp)

    v = own_f(0) + gf[z, xl].astype(F32)
    got(rfm.at[2], rfm_r.at[2])
    got(rfp.at[3], rfp_r.at[3])
    hf[...] = (v + rfm[2].astype(F32) + rfp[3].astype(F32)).astype(BF16)
    put(hf, out_f.at[0], ho_s.at[0], ho_r.at[0], nxt)

    v = pb[z, xl] + rbp[2, xl].astype(F32) + rbm[3, xl].astype(F32) + gb[z, xl].astype(F32)
    got(rxb, rx_r.at[0])
    hbk[...] = (v + rxb[...].astype(F32)).astype(BF16)
    put(hbk, out_b.at[0], ho_s.at[1], ho_r.at[1], prv)

    cp_g.wait()
    for cp in sent:
        cp.wait_send()
    got(out_f.at[0], ho_r.at[0])
    got(out_b.at[0], ho_r.at[1])


def shards(inputs, gate_pre, up_weight, down_weight, output_grad):
    vm = pltpu.VMEM
    dma = lambda n: [pltpu.SemaphoreType.DMA((n,)), pltpu.SemaphoreType.DMA((n,))]
    blk = lambda *n: vm((*n, 8, 2048), BF16)
    mat = lambda t: vm((128, 896), t)
    any_spec = pl.BlockSpec(memory_space=pl.ANY)
    return pl.pallas_call(
        kernel,
        out_shape=(
            jax.ShapeDtypeStruct((1, 8, 2048), BF16),
            jax.ShapeDtypeStruct((1, 64, 896), BF16),
            jax.ShapeDtypeStruct((1, 8, 2048), BF16),
        ),
        in_specs=[any_spec] * 5,
        out_specs=(any_spec,) * 3,
        scratch_shapes=[
            blk(8, 2), blk(8, 2), vm((2048, 896), BF16), vm((896, 2048), BF16), mat(BF16), mat(F32), mat(F32),
            mat(F32), mat(F32), mat(BF16), mat(BF16), mat(BF16), mat(BF16), vm((64, 896), BF16),
            vm((8, 2, 8, 2048), F32), vm((8, 2, 8, 2048), F32),
            blk(8), blk(8), blk(4), blk(4), blk(3), blk(3), blk(3, 2), blk(3, 2), blk(4, 2), blk(4, 2),
            blk(), blk(), blk(), blk(),
            pltpu.SemaphoreType.DMA((5,)),
            *dma(4), *dma(3), *dma(8), *dma(6), *dma(8), *dma(1),
            *dma(4), *dma(8), *dma(4), *dma(3), *dma(3), *dma(4), *dma(1), *dma(2),
        ],
        compiler_params=pltpu.CompilerParams(
            collective_id=0, has_side_effects=True, vmem_limit_bytes=60 * 1024 * 1024
        ),
        name="ffn",
    )(inputs, gate_pre, up_weight, down_weight, output_grad)


def solution(mesh):
    placed = (
        P("section", "col", "row"),
        P("section", None, "col"),
        P("row", "col"),
        P("col", "row"),
        P("section", "col", "row"),
    )
    return jax.shard_map(
        shards,
        mesh=mesh,
        in_specs=placed,
        out_specs=(
            P("section", "col", "row"),
            P("section", "row", "col"),
            P("section", "col", "row"),
        ),
        check_vma=False,
    )
```

```python
import jax
import jax.numpy as jnp
from jax import lax
from jax.experimental import pallas as pl
from jax.experimental.pallas import tpu as pltpu
from jax.sharding import PartitionSpec as P

MESH = pl.DeviceIdType.MESH
F32 = jnp.float32
BF16 = jnp.bfloat16
NT = (((1,), (1,)), ((), ()))
NN = (((1,), (0,)), ((), ()))
CUTS = ((0, 512), (512, 384))
B_LEN = (4, 3)
F_LEN = (3, 4)


def kernel(
    in_f, gate_in, up_in, dn_in, in_b,
    out_f, out_g, out_b,
    gf, gb, upv, dnv, gv, gs, dg,
    uf, hb, s1f, r1f, s1b, r1b, gg,
    pf, pb, sfp, rfp, sfm, rfm, sbp, rbp, sbm, rbm, sxf, rxf, sxb, rxb,
    m1f, n1f, m1b, n1b, mf, mb, of, ob,
    lsem, near, far, afp_s, afp_r, afm_s, afm_r, abp_s, abp_r, abm_s, abm_r, ax_s, ax_r,
    e_s, e_r, rfp_s, rfp_r, rfm_s, rfm_r, rbp_s, rbp_r, rbm_s, rbm_r, rx_s, rx_r,
    h1_s, h1_r, hf_s, hf_r, hb_s, hb_r,
):
    s = lax.axis_index("section")
    r = lax.axis_index("row")
    c = lax.axis_index("col")
    z, xl = c // 2, c % 2
    xo = 1 - xl
    ns = lax.axis_size("section")
    sp, sm = (s + 1) % ns, (s + ns - 1) % ns
    up1, dn1 = (z + 1) % 8, (z + 7) % 8
    zp = {"col": up1 * 2 + xl}
    zm = {"col": dn1 * 2 + xl}
    xp = {"col": z * 2 + xo}
    mate = {"row": 1 - r}

    def at(sec, zz, x):
        return {"section": sec, "col": zz * 2 + x}

    def fetch(src, dst, i):
        cp = pltpu.make_async_copy(src, dst, lsem.at[i])
        cp.start()
        return cp

    cp_gate = fetch(gate_in.at[0], gv, 0)
    cp_f = fetch(in_f.at[0], gf.at[z, xl], 1)
    cp_b = fetch(in_b.at[0], gb.at[z, xl], 2)
    cp_dn = fetch(dn_in, dnv, 4)
    cp_up = fetch(up_in, upv, 3)

    barrier = pltpu.get_barrier_semaphore()
    greet = [xp, mate, zm]
    for sec in (sp, sm):
        greet += [at(sec, z, xl), at(sec, dn1, xl), at(sec, dn1, xo)]
    for dev in greet:
        pl.semaphore_signal(barrier, inc=1, device_id=dev, device_id_type=MESH)
    pl.semaphore_wait(barrier, 9)

    sent = []

    def rc(src, dst, ss, rs, dev):
        return pltpu.make_async_remote_copy(
            src_ref=src, dst_ref=dst, send_sem=ss, recv_sem=rs, device_id=dev, device_id_type=MESH
        )

    def put(src, dst, ss, rs, dev, keep=True):
        cp = rc(src, dst, ss, rs, dev)
        cp.start()
        if keep:
            sent.append(cp)

    def got(dst, rs):
        rc(dst, dst, rs, rs, zp).wait_recv()

    pl.semaphore_signal(near, inc=1, device_id=zp, device_id_type=MESH)
    put(in_b.at[0], gb.at[z, xl], ax_s.at[0], ax_r.at[0], xp)
    put(in_f.at[0], gf.at[z, xl], ax_s.at[1], ax_r.at[1], xp)
    for sec in (sp, sm):
        for x in (xl, xo):
            pl.semaphore_signal(far, inc=1, device_id=at(sec, up1, x), device_id_type=MESH)

    plus = {0: (gb, abp_s, abp_r, B_LEN[0]), 1: (gf, afp_s, afp_r, F_LEN[0])}
    minus = {0: (gb, abm_s, abm_r, B_LEN[1]), 1: (gf, afm_s, afm_r, F_LEN[1])}

    def send_plus(t, d, o):
        buf, ss, rs, _ = plus[t]
        put(buf.at[o], buf.at[o], ss.at[d], rs.at[d], zp, False)

    def send_minus(t, d, o):
        buf, ss, rs, _ = minus[t]
        put(buf.at[o], buf.at[o], ss.at[d], rs.at[d], zm, False)

    def recv_plus(t, keep):
        buf, ss, rs, n = plus[t]
        for d in range(1, n + 1):
            def step(d=d):
                o = (z + 8 - d) % 8
                got(buf.at[o], rs.at[d - 1])
                if d < n:
                    send_plus(t, d, o)
            pl.when(keep(d))(step)

    def recv_minus(t, keep):
        buf, ss, rs, n = minus[t]
        for d in range(1, n + 1):
            def step(d=d):
                o = (z + d) % 8
                got(buf.at[o], rs.at[d - 1])
                if d < n:
                    send_minus(t, d, o)
            pl.when(keep(d))(step)

    cp_b.wait()
    got(gb.at[z, xo], ax_r.at[0])
    send_plus(0, 0, z)
    cp_f.wait()
    got(gf.at[z, xo], ax_r.at[1])

    @pl.when(z > 0)
    def _():
        pl.semaphore_wait(near, 1)
        send_minus(0, 0, z)
        send_minus(1, 0, z)

    cp_gate.wait()
    g32 = gv[...].astype(F32)
    sg = 1.0 / (1.0 + jnp.exp(-g32))
    gs[...] = g32 * sg
    dg[...] = sg * (1.0 + g32 * (1.0 - sg))

    recv_plus(0, lambda d: d <= z)
    send_plus(1, 0, z)
    recv_plus(1, lambda d: (d <= z) & (z < 7))

    @pl.when(z == 0)
    def _():
        pl.semaphore_wait(near, 1)
        send_minus(0, 0, z)

    recv_minus(0, lambda d: d <= 7 - z)

    @pl.when(z == 0)
    def _():
        send_minus(1, 0, z)

    recv_minus(1, lambda d: d <= 7 - z)
    recv_plus(0, lambda d: d > z)
    recv_minus(0, lambda d: d > 7 - z)

    cp_dn.wait()
    grd = gb[...].reshape(128, 2048)
    for i, (a, w) in enumerate(CUTS):
        v = lax.dot_general(grd, dnv[a : a + w, :], NT, preferred_element_type=F32)
        hb[:, a : a + w] = v
        s1b[:, a : a + w] = v.astype(BF16)
        put(s1b.at[:, a : a + w], r1b.at[:, a : a + w], e_s.at[2 + i], e_r.at[2 + i], mate)

    recv_plus(1, lambda d: (d > z) | (z == 7))
    recv_minus(1, lambda d: d > 7 - z)

    cp_up.wait()
    act = gf[...].reshape(128, 2048)
    for i, (a, w) in enumerate(CUTS):
        v = lax.dot_general(act, upv[:, a : a + w], NN, preferred_element_type=F32)
        uf[:, a : a + w] = v
        s1f[:, a : a + w] = v.astype(BF16)
        put(s1f.at[:, a : a + w], r1f.at[:, a : a + w], e_s.at[i], e_r.at[i], mate)

    chains = {
        (0, 0): (pb, sbp, rbp, rbp_s, rbp_r, B_LEN[0]),
        (0, 1): (pb, sbm, rbm, rbm_s, rbm_r, B_LEN[1]),
        (1, 0): (pf, sfp, rfp, rfp_s, rfp_r, F_LEN[0]),
        (1, 1): (pf, sfm, rfm, rfm_s, rfm_r, F_LEN[1]),
    }
    ends = {0: (mb, hb_s, hb_r, sm), 1: (mf, hf_s, hf_r, sp)}

    def chain(t, way, k):
        part, snd, rcv, ss, rs, n = chains[t, way]
        if k >= n:
            return
        d = n - k
        target = (z + d) % 8 if way == 0 else (z + 8 - d) % 8
        v = part[target]
        if k > 0:
            got(rcv.at[k - 1], rs.at[k - 1])
            v = v + rcv[k - 1].astype(F32)
        snd[k] = v.astype(BF16)
        if d > 1:
            put(snd.at[k], rcv.at[k], ss.at[k], rs.at[k], zp if way == 0 else zm)
        else:
            land, fs, fr, sec = ends[t]
            for j, x in enumerate((xl, xo)):
                i = way * 2 + j
                put(snd.at[k, x], land.at[i], fs.at[i], fr.at[i], at(sec, target, x))

    def share(t, part, snd, rcv):
        snd[...] = part[z, xo].astype(BF16)
        put(snd, rcv, rx_s.at[t], rx_r.at[t], xp)

    def hand(t, part, rcv, buf, m, n, sec):
        got(rcv, rx_r.at[t])
        m[...] = part[z, xl] + buf[z, xl].astype(F32) + rcv[...].astype(F32)
        put(m, n, h1_s.at[t], h1_r.at[t], at(sec, z, xl))

    for i, (a, w) in enumerate(CUTS):
        got(r1b.at[:, a : a + w], e_r.at[2 + i])
    h = hb[...] + r1b[...].astype(F32)
    hb[...] = h
    upg = (gs[...] * h).astype(BF16)
    for a in range(0, 2048, 512):
        v = lax.dot_general(upg, upv[a : a + 512, :], NT, preferred_element_type=F32)
        pb[:, :, :, a : a + 512] = v.reshape(8, 2, 8, 512)
    chain(0, 0, 0)
    chain(0, 1, 0)
    share(0, pb, sxb, rxb)

    for i, (a, w) in enumerate(CUTS):
        got(r1f.at[:, a : a + w], e_r.at[i])
    u = uf[...] + r1f[...].astype(F32)
    uf[...] = u
    hid = (gs[...] * u).astype(BF16)
    for a in range(0, 2048, 512):
        v = lax.dot_general(hid, dnv[:, a : a + 512], NN, preferred_element_type=F32)
        pf[:, :, :, a : a + 512] = v.reshape(8, 2, 8, 512)
    chain(1, 1, 0)
    chain(1, 0, 0)
    share(1, pf, sxf, rxf)

    chain(0, 0, 1)
    chain(0, 1, 1)
    hand(0, pb, rxb, gb, m1b, n1b, sm)
    rows = pl.ds(pl.multiple_of(r * 64, 64), 64)
    gg[...] = (hb[rows, :] * uf[rows, :] * dg[rows, :]).astype(BF16)
    cp_g = fetch(gg, out_g.at[0], 0)
    chain(1, 1, 1)
    chain(1, 0, 1)
    hand(1, pf, rxf, gf, m1f, n1f, sp)
    pl.semaphore_wait(far, 4)
    chain(0, 0, 2)
    chain(0, 1, 2)
    chain(1, 1, 2)
    chain(1, 0, 2)
    chain(0, 0, 3)
    chain(1, 1, 3)

    for t, (n1, land, fr, o, out) in enumerate(((n1b, mb, hb_r, ob, out_b), (n1f, mf, hf_r, of, out_f))):
        got(n1, h1_r.at[t])
        v = n1[...]
        for i in (2, 3, 0, 1):
            got(land.at[i], fr.at[i])
            v = v + land[i].astype(F32)
        o[...] = v.astype(BF16)
        fetch(o, out.at[0], 1 + t)

    for cp in sent:
        cp.wait_send()
    for t in (0, 1):
        for (buf, ss, rs, n), dev in ((plus[t], zp), (minus[t], zm)):
            for d in range(n):
                rc(buf.at[z], buf.at[z], ss.at[d], rs.at[d], dev).wait_send()
    cp_g.wait()
    pltpu.make_async_copy(ob, out_b.at[0], lsem.at[1]).wait()
    pltpu.make_async_copy(of, out_f.at[0], lsem.at[2]).wait()


def writer(a, b, c, x, y, w, av, bv, cv, isem, osem):
    trio = ((a, av, x), (b, bv, y), (c, cv, w))
    loads = [pltpu.make_async_copy(p, v, isem.at[i]) for i, (p, v, _) in enumerate(trio)]
    for cp in loads:
        cp.start()
    stores = [pltpu.make_async_copy(v, q, osem.at[i]) for i, (_, v, q) in enumerate(trio)]
    for i in range(3):
        loads[i].wait()
        stores[i].start()
    for cp in stores:
        cp.wait()


def shards(inputs, gate_pre, up_weight, down_weight, output_grad):
    vm = pltpu.VMEM
    dma = lambda n: [pltpu.SemaphoreType.DMA((n,)), pltpu.SemaphoreType.DMA((n,))]
    blk = lambda *n: vm((*n, 8, 2048), BF16)
    wide = lambda: vm((8, 2048), F32)
    mat = lambda t: vm((128, 896), t)
    any_spec = pl.BlockSpec(memory_space=pl.ANY)
    shapes = (
        jax.ShapeDtypeStruct((1, 8, 2048), BF16),
        jax.ShapeDtypeStruct((1, 64, 896), BF16),
        jax.ShapeDtypeStruct((1, 8, 2048), BF16),
    )
    results = pl.pallas_call(
        kernel,
        out_shape=shapes,
        in_specs=[any_spec] * 5,
        out_specs=(any_spec,) * 3,
        scratch_shapes=[
            blk(8, 2), blk(8, 2), vm((2048, 896), BF16), vm((896, 2048), BF16), mat(BF16), mat(F32), mat(F32),
            mat(F32), mat(F32), mat(BF16), mat(BF16), mat(BF16), mat(BF16), vm((64, 896), BF16),
            vm((8, 2, 8, 2048), F32), vm((8, 2, 8, 2048), F32),
            blk(3, 2), blk(2, 2), blk(4, 2), blk(3, 2), blk(4, 2), blk(3, 2), blk(3, 2), blk(2, 2),
            blk(), blk(), blk(), blk(),
            wide(), wide(), wide(), wide(), blk(4), blk(4), blk(), blk(),
            pltpu.SemaphoreType.DMA((5,)), pltpu.SemaphoreType.REGULAR, pltpu.SemaphoreType.REGULAR,
            *dma(F_LEN[0]), *dma(F_LEN[1]), *dma(B_LEN[0]), *dma(B_LEN[1]), *dma(2),
            *dma(4), *dma(F_LEN[0]), *dma(F_LEN[1]), *dma(B_LEN[0]), *dma(B_LEN[1]), *dma(2),
            *dma(2), *dma(4), *dma(4),
        ],
        compiler_params=pltpu.CompilerParams(
            collective_id=0, has_side_effects=True, vmem_limit_bytes=60 * 1024 * 1024
        ),
        name="ffn",
    )(inputs, gate_pre, up_weight, down_weight, output_grad)
    return pl.pallas_call(
        writer,
        out_shape=shapes,
        in_specs=[any_spec] * 3,
        out_specs=(any_spec,) * 3,
        scratch_shapes=[
            vm((1, 8, 2048), BF16), vm((1, 64, 896), BF16), vm((1, 8, 2048), BF16),
            pltpu.SemaphoreType.DMA((3,)), pltpu.SemaphoreType.DMA((3,)),
        ],
        name="write",
    )(*results)


def solution(mesh):
    placed = (
        P("section", "col", "row"),
        P("section", None, "col"),
        P("row", "col"),
        P("col", "row"),
        P("section", "col", "row"),
    )
    return jax.shard_map(
        shards,
        mesh=mesh,
        in_specs=placed,
        out_specs=(
            P("section", "col", "row"),
            P("section", "row", "col"),
            P("section", "col", "row"),
        ),
        check_vma=False,
    )
```

```python
import jax
import jax.numpy as jnp
from jax import lax
from jax.experimental import pallas as pl
from jax.experimental.pallas import tpu as pltpu
from jax.sharding import PartitionSpec as P

MESH = pl.DeviceIdType.MESH
F32 = jnp.float32
BF16 = jnp.bfloat16
NT = (((1,), (1,)), ((), ()))
NN = (((1,), (0,)), ((), ()))
CUTS = ((0, 512), (512, 384))
B_LEN = (4, 3)
F_LEN = (3, 4)


def kernel(
    in_f, gate_in, up_in, dn_in, in_b,
    out_f, out_g, out_b,
    gf, gb, upv, dnv, gv, gs, dg,
    uf, hb, s1f, r1f, s1b, r1b, gg,
    pf, pb, sfp, rfp, sfm, rfm, sbp, rbp, sbm, rbm, sxf, rxf, sxb, rxb,
    m1f, n1f, m1b, n1b, mf, mb, of, ob,
    lsem, near, far, fzp_s, fzp_r, fzm_s, fzm_r, fx_s, fx_r, bzp_s, bzp_r, bzm_s, bzm_r, bx_s, bx_r,
    e_s, e_r, rfp_s, rfp_r, rfm_s, rfm_r, rbp_s, rbp_r, rbm_s, rbm_r, rx_s, rx_r,
    h1_s, h1_r, hf_s, hf_r, hb_s, hb_r,
):
    s = lax.axis_index("section")
    r = lax.axis_index("row")
    c = lax.axis_index("col")
    z, xl = c // 2, c % 2
    xo = 1 - xl
    ns = lax.axis_size("section")
    sp, sm = (s + 1) % ns, (s + ns - 1) % ns
    up1, dn1 = (z + 1) % 8, (z + 7) % 8
    zp = {"col": up1 * 2 + xl}
    zm = {"col": dn1 * 2 + xl}
    xp = {"col": z * 2 + xo}
    mate = {"row": 1 - r}

    def at(sec, zz, x):
        return {"section": sec, "col": zz * 2 + x}

    def fetch(src, dst, i):
        cp = pltpu.make_async_copy(src, dst, lsem.at[i])
        cp.start()
        return cp

    cp_gate = fetch(gate_in.at[0], gv, 0)
    cp_f = fetch(in_f.at[0], gf.at[z, xl], 1)
    cp_b = fetch(in_b.at[0], gb.at[z, xl], 2)
    cp_dn = fetch(dn_in, dnv, 4)
    cp_up = fetch(up_in, upv, 3)

    barrier = pltpu.get_barrier_semaphore()
    for dev in (zp, zm, xp, mate):
        pl.semaphore_signal(barrier, inc=1, device_id=dev, device_id_type=MESH)

    @pl.when(z == 0)
    def _():
        for sec in (sp, sm):
            pl.semaphore_signal(barrier, inc=1, device_id={"section": sec}, device_id_type=MESH)
        pl.semaphore_wait(barrier, 6)

    @pl.when(z > 0)
    def _():
        pl.semaphore_wait(barrier, 4)

    sent = []

    def rc(src, dst, ss, rs, dev):
        return pltpu.make_async_remote_copy(
            src_ref=src, dst_ref=dst, send_sem=ss, recv_sem=rs, device_id=dev, device_id_type=MESH
        )

    def put(src, dst, ss, rs, dev):
        cp = rc(src, dst, ss, rs, dev)
        cp.start()
        sent.append(cp)

    def got(dst, rs):
        rc(dst, dst, rs, rs, zp).wait_recv()

    put(in_b.at[0], gb.at[z, xl], bx_s.at[0], bx_r.at[0], xp)
    put(in_f.at[0], gf.at[z, xl], fzp_s.at[0], fzp_r.at[0], zp)
    put(in_f.at[0], gf.at[z, xl], fzm_s.at[0], fzm_r.at[0], zm)
    put(in_b.at[0], gb.at[z, xl], bzp_s.at[0], bzp_r.at[0], zp)
    put(in_b.at[0], gb.at[z, xl], bzm_s.at[0], bzm_r.at[0], zm)
    put(in_f.at[0], gf.at[z, xl], fx_s.at[0], fx_r.at[0], xp)

    cp_gate.wait()
    g32 = gv[...].astype(F32)
    sg = 1.0 / (1.0 + jnp.exp(-g32))
    gs[...] = g32 * sg
    dg[...] = sg * (1.0 + g32 * (1.0 - sg))

    got(gb.at[z, xo], bx_r.at[0])
    put(gb.at[z, xo], gb.at[z, xo], bzp_s.at[3], bzp_r.at[3], zp)
    put(gb.at[z, xo], gb.at[z, xo], bzm_s.at[4], bzm_r.at[4], zm)
    for d in range(1, 5):
        lo, hi = (z + 8 - d) % 8, (z + d) % 8
        got(gf.at[lo, xl], fzp_r.at[d - 1])
        if d < 4:
            put(gf.at[lo, xl], gf.at[lo, xl], fzp_s.at[d], fzp_r.at[d], zp)
        put(gf.at[lo, xl], gf.at[lo, xl], fx_s.at[d], fx_r.at[d], xp)
        if d <= 3:
            got(gf.at[hi, xl], fzm_r.at[d - 1])
            if d < 3:
                put(gf.at[hi, xl], gf.at[hi, xl], fzm_s.at[d], fzm_r.at[d], zm)
            put(gf.at[hi, xl], gf.at[hi, xl], fx_s.at[4 + d], fx_r.at[4 + d], xp)
        for half, x in ((0, xl), (1, xo)):
            if d <= 3:
                i = half * 3 + d - 1
                got(gb.at[lo, x], bzp_r.at[i])
                if d < 3:
                    put(gb.at[lo, x], gb.at[lo, x], bzp_s.at[i + 1], bzp_r.at[i + 1], zp)
            i = half * 4 + d - 1
            got(gb.at[hi, x], bzm_r.at[i])
            if d < 4:
                put(gb.at[hi, x], gb.at[hi, x], bzm_s.at[i + 1], bzm_r.at[i + 1], zm)
    got(gf.at[z, xo], fx_r.at[0])
    for d in range(1, 5):
        got(gf.at[(z + 8 - d) % 8, xo], fx_r.at[d])
        if d <= 3:
            got(gf.at[(z + d) % 8, xo], fx_r.at[4 + d])
    cp_f.wait()
    cp_b.wait()

    @pl.when(z == 0)
    def _():
        for sec in (sp, sm):
            pl.semaphore_signal(far, inc=1, device_id={"section": sec}, device_id_type=MESH)

    cp_up.wait()
    act = gf[...].reshape(128, 2048)
    for i, (a, w) in enumerate(CUTS):
        v = lax.dot_general(act, upv[:, a : a + w], NN, preferred_element_type=F32)
        uf[:, a : a + w] = v
        s1f[:, a : a + w] = v.astype(BF16)
        put(s1f.at[:, a : a + w], r1f.at[:, a : a + w], e_s.at[i], e_r.at[i], mate)

    cp_dn.wait()
    grd = gb[...].reshape(128, 2048)
    for i, (a, w) in enumerate(CUTS):
        v = lax.dot_general(grd, dnv[a : a + w, :], NT, preferred_element_type=F32)
        hb[:, a : a + w] = v
        s1b[:, a : a + w] = v.astype(BF16)
        put(s1b.at[:, a : a + w], r1b.at[:, a : a + w], e_s.at[2 + i], e_r.at[2 + i], mate)

    chains = {
        (0, 0): (pb, sbp, rbp, rbp_s, rbp_r, B_LEN[0]),
        (0, 1): (pb, sbm, rbm, rbm_s, rbm_r, B_LEN[1]),
        (1, 0): (pf, sfp, rfp, rfp_s, rfp_r, F_LEN[0]),
        (1, 1): (pf, sfm, rfm, rfm_s, rfm_r, F_LEN[1]),
    }
    ends = {0: (mb, hb_s, hb_r, sm), 1: (mf, hf_s, hf_r, sp)}

    def chain(t, way, k):
        part, snd, rcv, ss, rs, n = chains[t, way]
        if k >= n:
            return
        d = n - k
        target = (z + d) % 8 if way == 0 else (z + 8 - d) % 8
        for j, x in enumerate((xl, xo)):
            v = part[target, x]
            if k > 0:
                got(rcv.at[k - 1, x], rs.at[2 * k - 2 + j])
                v = v + rcv[k - 1, x].astype(F32)
            snd[k, x] = v.astype(BF16)
            if d > 1:
                put(snd.at[k, x], rcv.at[k, x], ss.at[2 * k + j], rs.at[2 * k + j], zp if way == 0 else zm)
            else:
                land, fs, fr, sec = ends[t]
                i = way * 2 + j
                put(snd.at[k, x], land.at[i], fs.at[i], fr.at[i], at(sec, target, x))

    def share(t, part, snd, rcv):
        snd[...] = part[z, xo].astype(BF16)
        put(snd, rcv, rx_s.at[t], rx_r.at[t], xp)

    def hand(t, part, rcv, buf, m, n, sec):
        got(rcv, rx_r.at[t])
        m[...] = part[z, xl] + buf[z, xl].astype(F32) + rcv[...].astype(F32)
        put(m, n, h1_s.at[t], h1_r.at[t], at(sec, z, xl))

    for i, (a, w) in enumerate(CUTS):
        got(r1f.at[:, a : a + w], e_r.at[i])
    u = uf[...] + r1f[...].astype(F32)
    uf[...] = u
    hid = (gs[...] * u).astype(BF16)
    for a in range(0, 2048, 512):
        v = lax.dot_general(hid, dnv[:, a : a + 512], NN, preferred_element_type=F32)
        pf[:, :, :, a : a + 512] = v.reshape(8, 2, 8, 512)
    share(1, pf, sxf, rxf)
    chain(1, 1, 0)
    chain(1, 0, 0)

    for i, (a, w) in enumerate(CUTS):
        got(r1b.at[:, a : a + w], e_r.at[2 + i])
    h = hb[...] + r1b[...].astype(F32)
    hb[...] = h
    upg = (gs[...] * h).astype(BF16)
    for a in range(0, 2048, 512):
        v = lax.dot_general(upg, upv[a : a + 512, :], NT, preferred_element_type=F32)
        pb[:, :, :, a : a + 512] = v.reshape(8, 2, 8, 512)
    share(0, pb, sxb, rxb)
    chain(0, 0, 0)
    chain(0, 1, 0)

    chain(1, 1, 1)
    chain(1, 0, 1)

    @pl.when(z == 0)
    def _():
        pl.semaphore_wait(far, 2)
        for k in range(1, 8):
            pl.semaphore_signal(near, inc=1, device_id={"col": k * 2 + xl}, device_id_type=MESH)

    rows = pl.ds(pl.multiple_of(r * 64, 64), 64)
    gg[...] = (hb[rows, :] * uf[rows, :] * dg[rows, :]).astype(BF16)
    cp_g = fetch(gg, out_g.at[0], 0)
    chain(0, 0, 1)
    chain(0, 1, 1)

    @pl.when(z > 0)
    def _():
        pl.semaphore_wait(near, 1)

    chain(1, 1, 2)
    chain(1, 0, 2)
    hand(1, pf, rxf, gf, m1f, n1f, sp)
    chain(0, 0, 2)
    chain(0, 1, 2)
    hand(0, pb, rxb, gb, m1b, n1b, sm)
    chain(1, 1, 3)
    chain(0, 0, 3)

    for t, (n1, land, fr, o, out) in ((1, (n1f, mf, hf_r, of, out_f)), (0, (n1b, mb, hb_r, ob, out_b))):
        got(n1, h1_r.at[t])
        v = n1[...]
        for i in (2, 3, 0, 1):
            got(land.at[i], fr.at[i])
            v = v + land[i].astype(F32)
        o[...] = v.astype(BF16)
        fetch(o, out.at[0], 1 + t)

    for cp in sent:
        cp.wait_send()
    cp_g.wait()
    pltpu.make_async_copy(ob, out_b.at[0], lsem.at[1]).wait()
    pltpu.make_async_copy(of, out_f.at[0], lsem.at[2]).wait()


def writer(a, b, c, x, y, w, av, bv, cv, isem, osem):
    trio = ((a, av, x), (b, bv, y), (c, cv, w))
    loads = [pltpu.make_async_copy(p, v, isem.at[i]) for i, (p, v, _) in enumerate(trio)]
    for cp in loads:
        cp.start()
    stores = [pltpu.make_async_copy(v, q, osem.at[i]) for i, (_, v, q) in enumerate(trio)]
    for i in range(3):
        loads[i].wait()
        stores[i].start()
    for cp in stores:
        cp.wait()


def shards(inputs, gate_pre, up_weight, down_weight, output_grad):
    vm = pltpu.VMEM
    dma = lambda n: [pltpu.SemaphoreType.DMA((n,)), pltpu.SemaphoreType.DMA((n,))]
    blk = lambda *n: vm((*n, 8, 2048), BF16)
    wide = lambda: vm((8, 2048), F32)
    mat = lambda t: vm((128, 896), t)
    any_spec = pl.BlockSpec(memory_space=pl.ANY)
    shapes = (
        jax.ShapeDtypeStruct((1, 8, 2048), BF16),
        jax.ShapeDtypeStruct((1, 64, 896), BF16),
        jax.ShapeDtypeStruct((1, 8, 2048), BF16),
    )
    results = pl.pallas_call(
        kernel,
        out_shape=shapes,
        in_specs=[any_spec] * 5,
        out_specs=(any_spec,) * 3,
        scratch_shapes=[
            blk(8, 2), blk(8, 2), vm((2048, 896), BF16), vm((896, 2048), BF16), mat(BF16), mat(F32), mat(F32),
            mat(F32), mat(F32), mat(BF16), mat(BF16), mat(BF16), mat(BF16), vm((64, 896), BF16),
            vm((8, 2, 8, 2048), F32), vm((8, 2, 8, 2048), F32),
            blk(3, 2), blk(2, 2), blk(4, 2), blk(3, 2), blk(4, 2), blk(3, 2), blk(3, 2), blk(2, 2),
            blk(), blk(), blk(), blk(),
            wide(), wide(), wide(), wide(), blk(4), blk(4), blk(), blk(),
            pltpu.SemaphoreType.DMA((5,)), pltpu.SemaphoreType.REGULAR, pltpu.SemaphoreType.REGULAR,
            *dma(4), *dma(3), *dma(8), *dma(6), *dma(8), *dma(1),
            *dma(4), *dma(2 * F_LEN[0]), *dma(2 * F_LEN[1]), *dma(2 * B_LEN[0]), *dma(2 * B_LEN[1]), *dma(2),
            *dma(2), *dma(4), *dma(4),
        ],
        compiler_params=pltpu.CompilerParams(
            collective_id=0, has_side_effects=True, vmem_limit_bytes=60 * 1024 * 1024
        ),
        name="ffn",
    )(inputs, gate_pre, up_weight, down_weight, output_grad)
    return pl.pallas_call(
        writer,
        out_shape=shapes,
        in_specs=[any_spec] * 3,
        out_specs=(any_spec,) * 3,
        scratch_shapes=[
            vm((1, 8, 2048), BF16), vm((1, 64, 896), BF16), vm((1, 8, 2048), BF16),
            pltpu.SemaphoreType.DMA((3,)), pltpu.SemaphoreType.DMA((3,)),
        ],
        name="write",
    )(*results)


def solution(mesh):
    placed = (
        P("section", "col", "row"),
        P("section", None, "col"),
        P("row", "col"),
        P("col", "row"),
        P("section", "col", "row"),
    )
    return jax.shard_map(
        shards,
        mesh=mesh,
        in_specs=placed,
        out_specs=(
            P("section", "col", "row"),
            P("section", "row", "col"),
            P("section", "col", "row"),
        ),
        check_vma=False,
    )
```

```python
import jax
import jax.numpy as jnp
from jax import lax
from jax.experimental import pallas as pl
from jax.experimental.pallas import tpu as pltpu
from jax.sharding import PartitionSpec as P

MESH = pl.DeviceIdType.MESH
F32 = jnp.float32
BF16 = jnp.bfloat16
NT = (((1,), (1,)), ((), ()))
NN = (((1,), (0,)), ((), ()))
CUTS = ((0, 512), (512, 384))
B_LEN = (4, 3)
F_LEN = (3, 4)


def kernel(
    in_f, gate_in, up_in, dn_in, in_b,
    out_f, out_g, out_b,
    gf, gb, upv, dnv, gv, gs, dg,
    uf, hb, s1f, r1f, s1b, r1b,
    pf, pb, sfp, rfp, sfm, rfm, sbp, rbp, sbm, rbm, sxf, rxf, sxb, rxb,
    m1f, n1f, m1b, n1b, mf, mb,
    lsem, near, far, fzp_s, fzp_r, fzm_s, fzm_r, fx_s, fx_r, bzp_s, bzp_r, bzm_s, bzm_r, bx_s, bx_r,
    e_s, e_r, rfp_s, rfp_r, rfm_s, rfm_r, rbp_s, rbp_r, rbm_s, rbm_r, rx_s, rx_r,
    h1_s, h1_r, hf_s, hf_r, hb_s, hb_r,
):
    s = lax.axis_index("section")
    r = lax.axis_index("row")
    c = lax.axis_index("col")
    z, xl = c // 2, c % 2
    xo = 1 - xl
    ns = lax.axis_size("section")
    sp, sm = (s + 1) % ns, (s + ns - 1) % ns
    up1, dn1 = (z + 1) % 8, (z + 7) % 8
    zp = {"col": up1 * 2 + xl}
    zm = {"col": dn1 * 2 + xl}
    xp = {"col": z * 2 + xo}
    mate = {"row": 1 - r}

    def at(sec, zz, x):
        return {"section": sec, "col": zz * 2 + x}

    def fetch(src, dst, i):
        cp = pltpu.make_async_copy(src, dst, lsem.at[i])
        cp.start()
        return cp

    cp_gate = fetch(gate_in.at[0], gv, 0)
    cp_f = fetch(in_f.at[0], gf.at[z, xl], 1)
    cp_b = fetch(in_b.at[0], gb.at[z, xl], 2)
    cp_dn = fetch(dn_in, dnv, 4)
    cp_up = fetch(up_in, upv, 3)

    barrier = pltpu.get_barrier_semaphore()
    for dev in (zp, zm, xp, mate):
        pl.semaphore_signal(barrier, inc=1, device_id=dev, device_id_type=MESH)

    @pl.when(z == 0)
    def _():
        for sec in (sp, sm):
            pl.semaphore_signal(barrier, inc=1, device_id={"section": sec}, device_id_type=MESH)
        pl.semaphore_wait(barrier, 6)

    @pl.when(z > 0)
    def _():
        pl.semaphore_wait(barrier, 4)

    sent = []

    def rc(src, dst, ss, rs, dev):
        return pltpu.make_async_remote_copy(
            src_ref=src, dst_ref=dst, send_sem=ss, recv_sem=rs, device_id=dev, device_id_type=MESH
        )

    def put(src, dst, ss, rs, dev):
        cp = rc(src, dst, ss, rs, dev)
        cp.start()
        sent.append(cp)

    def got(dst, rs):
        rc(dst, dst, rs, rs, zp).wait_recv()

    put(in_b.at[0], gb.at[z, xl], bx_s.at[0], bx_r.at[0], xp)
    put(in_f.at[0], gf.at[z, xl], fzp_s.at[0], fzp_r.at[0], zp)
    put(in_f.at[0], gf.at[z, xl], fzm_s.at[0], fzm_r.at[0], zm)
    put(in_b.at[0], gb.at[z, xl], bzp_s.at[0], bzp_r.at[0], zp)
    put(in_b.at[0], gb.at[z, xl], bzm_s.at[0], bzm_r.at[0], zm)
    put(in_f.at[0], gf.at[z, xl], fx_s.at[0], fx_r.at[0], xp)

    cp_gate.wait()
    g32 = gv[...].astype(F32)
    sg = 1.0 / (1.0 + jnp.exp(-g32))
    gs[...] = g32 * sg
    dg[...] = sg * (1.0 + g32 * (1.0 - sg))

    got(gb.at[z, xo], bx_r.at[0])
    put(gb.at[z, xo], gb.at[z, xo], bzp_s.at[3], bzp_r.at[3], zp)
    put(gb.at[z, xo], gb.at[z, xo], bzm_s.at[4], bzm_r.at[4], zm)
    for d in range(1, 5):
        lo, hi = (z + 8 - d) % 8, (z + d) % 8
        got(gf.at[lo, xl], fzp_r.at[d - 1])
        if d < 4:
            put(gf.at[lo, xl], gf.at[lo, xl], fzp_s.at[d], fzp_r.at[d], zp)
        put(gf.at[lo, xl], gf.at[lo, xl], fx_s.at[d], fx_r.at[d], xp)
        if d <= 3:
            got(gf.at[hi, xl], fzm_r.at[d - 1])
            if d < 3:
                put(gf.at[hi, xl], gf.at[hi, xl], fzm_s.at[d], fzm_r.at[d], zm)
            put(gf.at[hi, xl], gf.at[hi, xl], fx_s.at[4 + d], fx_r.at[4 + d], xp)
        for half, x in ((0, xl), (1, xo)):
            if d <= 3:
                i = half * 3 + d - 1
                got(gb.at[lo, x], bzp_r.at[i])
                if d < 3:
                    put(gb.at[lo, x], gb.at[lo, x], bzp_s.at[i + 1], bzp_r.at[i + 1], zp)
            i = half * 4 + d - 1
            got(gb.at[hi, x], bzm_r.at[i])
            if d < 4:
                put(gb.at[hi, x], gb.at[hi, x], bzm_s.at[i + 1], bzm_r.at[i + 1], zm)
    got(gf.at[z, xo], fx_r.at[0])
    for d in range(1, 5):
        got(gf.at[(z + 8 - d) % 8, xo], fx_r.at[d])
        if d <= 3:
            got(gf.at[(z + d) % 8, xo], fx_r.at[4 + d])
    cp_f.wait()
    cp_b.wait()

    @pl.when(z == 0)
    def _():
        for sec in (sp, sm):
            pl.semaphore_signal(far, inc=1, device_id={"section": sec}, device_id_type=MESH)

    cp_up.wait()
    act = gf[...].reshape(128, 2048)
    for i, (a, w) in enumerate(CUTS):
        v = lax.dot_general(act, upv[:, a : a + w], NN, preferred_element_type=F32)
        uf[:, a : a + w] = v
        s1f[:, a : a + w] = v.astype(BF16)
        put(s1f.at[:, a : a + w], r1f.at[:, a : a + w], e_s.at[i], e_r.at[i], mate)

    cp_dn.wait()
    grd = gb[...].reshape(128, 2048)
    for i, (a, w) in enumerate(CUTS):
        v = lax.dot_general(grd, dnv[a : a + w, :], NT, preferred_element_type=F32)
        hb[:, a : a + w] = v
        s1b[:, a : a + w] = v.astype(BF16)
        put(s1b.at[:, a : a + w], r1b.at[:, a : a + w], e_s.at[2 + i], e_r.at[2 + i], mate)

    chains = {
        (0, 0): (pb, sbp, rbp, rbp_s, rbp_r, B_LEN[0]),
        (0, 1): (pb, sbm, rbm, rbm_s, rbm_r, B_LEN[1]),
        (1, 0): (pf, sfp, rfp, rfp_s, rfp_r, F_LEN[0]),
        (1, 1): (pf, sfm, rfm, rfm_s, rfm_r, F_LEN[1]),
    }
    ends = {0: (mb, hb_s, hb_r, sm), 1: (mf, hf_s, hf_r, sp)}

    def chain(t, way, k):
        part, snd, rcv, ss, rs, n = chains[t, way]
        if k >= n:
            return
        d = n - k
        target = (z + d) % 8 if way == 0 else (z + 8 - d) % 8
        for j, x in enumerate((xl, xo)):
            v = part[target, x]
            if k > 0:
                got(rcv.at[k - 1, x], rs.at[2 * k - 2 + j])
                v = v + rcv[k - 1, x].astype(F32)
            snd[k, x] = v.astype(BF16)
            if d > 1:
                put(snd.at[k, x], rcv.at[k, x], ss.at[2 * k + j], rs.at[2 * k + j], zp if way == 0 else zm)
            else:
                land, fs, fr, sec = ends[t]
                i = way * 2 + j
                put(snd.at[k, x], land.at[i], fs.at[i], fr.at[i], at(sec, target, x))

    def share(t, part, snd, rcv):
        snd[...] = part[z, xo].astype(BF16)
        put(snd, rcv, rx_s.at[t], rx_r.at[t], xp)

    def hand(t, part, rcv, buf, m, n, sec):
        got(rcv, rx_r.at[t])
        m[...] = part[z, xl] + buf[z, xl].astype(F32) + rcv[...].astype(F32)
        put(m, n, h1_s.at[t], h1_r.at[t], at(sec, z, xl))

    for i, (a, w) in enumerate(CUTS):
        got(r1f.at[:, a : a + w], e_r.at[i])
    u = uf[...] + r1f[...].astype(F32)
    uf[...] = u
    hid = (gs[...] * u).astype(BF16)
    for a in range(0, 2048, 512):
        v = lax.dot_general(hid, dnv[:, a : a + 512], NN, preferred_element_type=F32)
        pf[:, :, :, a : a + 512] = v.reshape(8, 2, 8, 512)
    share(1, pf, sxf, rxf)
    chain(1, 1, 0)
    chain(1, 0, 0)

    for i, (a, w) in enumerate(CUTS):
        got(r1b.at[:, a : a + w], e_r.at[2 + i])
    h = hb[...] + r1b[...].astype(F32)
    hb[...] = h
    upg = (gs[...] * h).astype(BF16)
    for a in range(0, 2048, 512):
        v = lax.dot_general(upg, upv[a : a + 512, :], NT, preferred_element_type=F32)
        pb[:, :, :, a : a + 512] = v.reshape(8, 2, 8, 512)
    share(0, pb, sxb, rxb)
    chain(0, 0, 0)
    chain(0, 1, 0)

    chain(1, 1, 1)
    chain(1, 0, 1)

    @pl.when(z == 0)
    def _():
        pl.semaphore_wait(far, 2)
        for k in range(1, 8):
            pl.semaphore_signal(near, inc=1, device_id={"col": k * 2 + xl}, device_id_type=MESH)

    rows = pl.ds(pl.multiple_of(r * 64, 64), 64)
    out_g[0] = (hb[rows, :] * uf[rows, :] * dg[rows, :]).astype(BF16)
    chain(0, 0, 1)
    chain(0, 1, 1)

    @pl.when(z > 0)
    def _():
        pl.semaphore_wait(near, 1)

    chain(1, 1, 2)
    chain(1, 0, 2)
    hand(1, pf, rxf, gf, m1f, n1f, sp)
    chain(0, 0, 2)
    chain(0, 1, 2)
    hand(0, pb, rxb, gb, m1b, n1b, sm)
    chain(1, 1, 3)
    chain(0, 0, 3)

    for t, (n1, land, fr, out) in ((1, (n1f, mf, hf_r, out_f)), (0, (n1b, mb, hb_r, out_b))):
        got(n1, h1_r.at[t])
        v = n1[...]
        for i in (2, 3, 0, 1):
            got(land.at[i], fr.at[i])
            v = v + land[i].astype(F32)
        out[0] = v.astype(BF16)

    for cp in sent:
        cp.wait_send()


def writer(a, b, c, x, y, w, sem):
    stores = [pltpu.make_async_copy(p, q, sem.at[i]) for i, (p, q) in enumerate(((a, x), (b, y), (c, w)))]
    for cp in stores:
        cp.start()
    for cp in stores:
        cp.wait()


def shards(inputs, gate_pre, up_weight, down_weight, output_grad):
    vm = pltpu.VMEM
    dma = lambda n: [pltpu.SemaphoreType.DMA((n,)), pltpu.SemaphoreType.DMA((n,))]
    blk = lambda *n: vm((*n, 8, 2048), BF16)
    wide = lambda: vm((8, 2048), F32)
    mat = lambda t: vm((128, 896), t)
    any_spec = pl.BlockSpec(memory_space=pl.ANY)
    in_vmem = pl.BlockSpec(memory_space=pltpu.VMEM)
    shapes = (
        jax.ShapeDtypeStruct((1, 8, 2048), BF16),
        jax.ShapeDtypeStruct((1, 64, 896), BF16),
        jax.ShapeDtypeStruct((1, 8, 2048), BF16),
    )
    results = pl.pallas_call(
        kernel,
        out_shape=tuple(vm(x.shape, x.dtype) for x in shapes),
        in_specs=[any_spec] * 5,
        out_specs=(in_vmem,) * 3,
        scratch_shapes=[
            blk(8, 2), blk(8, 2), vm((2048, 896), BF16), vm((896, 2048), BF16), mat(BF16), mat(F32), mat(F32),
            mat(F32), mat(F32), mat(BF16), mat(BF16), mat(BF16), mat(BF16),
            vm((8, 2, 8, 2048), F32), vm((8, 2, 8, 2048), F32),
            blk(3, 2), blk(2, 2), blk(4, 2), blk(3, 2), blk(4, 2), blk(3, 2), blk(3, 2), blk(2, 2),
            blk(), blk(), blk(), blk(),
            wide(), wide(), wide(), wide(), blk(4), blk(4),
            pltpu.SemaphoreType.DMA((5,)), pltpu.SemaphoreType.REGULAR, pltpu.SemaphoreType.REGULAR,
            *dma(4), *dma(3), *dma(8), *dma(6), *dma(8), *dma(1),
            *dma(4), *dma(2 * F_LEN[0]), *dma(2 * F_LEN[1]), *dma(2 * B_LEN[0]), *dma(2 * B_LEN[1]), *dma(2),
            *dma(2), *dma(4), *dma(4),
        ],
        compiler_params=pltpu.CompilerParams(
            collective_id=0, has_side_effects=True, vmem_limit_bytes=60 * 1024 * 1024
        ),
        name="ffn",
    )(inputs, gate_pre, up_weight, down_weight, output_grad)
    return pl.pallas_call(
        writer,
        out_shape=shapes,
        in_specs=[in_vmem] * 3,
        out_specs=(any_spec,) * 3,
        scratch_shapes=[pltpu.SemaphoreType.DMA((3,))],
        name="write",
    )(*(pltpu.with_memory_space_constraint(x, pltpu.VMEM) for x in results))


def solution(mesh):
    placed = (
        P("section", "col", "row"),
        P("section", None, "col"),
        P("row", "col"),
        P("col", "row"),
        P("section", "col", "row"),
    )
    return jax.shard_map(
        shards,
        mesh=mesh,
        in_specs=placed,
        out_specs=(
            P("section", "col", "row"),
            P("section", "row", "col"),
            P("section", "col", "row"),
        ),
        check_vma=False,
    )
```

```python
import jax
import jax.numpy as jnp
from jax import lax
from jax.experimental import pallas as pl
from jax.experimental.pallas import tpu as pltpu
from jax.sharding import PartitionSpec as P

MESH = pl.DeviceIdType.MESH
F32 = jnp.float32
BF16 = jnp.bfloat16
NT = (((1,), (1,)), ((), ()))
NN = (((1,), (0,)), ((), ()))
CUTS = ((0, 512), (512, 384))
B_LEN = (4, 3)
F_LEN = (3, 4)


def kernel(
    in_f, gate_in, up_in, dn_in, in_b,
    out_f, out_g, out_b,
    gf, gb, upv, dnv, gv, gs, dg,
    uf, hb, s1f, r1f, s1b, r1b,
    pf, pb, sfp, rfp, sfm, rfm, sbp, rbp, sbm, rbm, sxf, rxf, sxb, rxb,
    m1f, n1f, m1b, n1b, mf, mb,
    lsem, near, far, fzp_s, fzp_r, fzm_s, fzm_r, fx_s, fx_r, bzp_s, bzp_r, bzm_s, bzm_r, bx_s, bx_r,
    e_s, e_r, rfp_s, rfp_r, rfm_s, rfm_r, rbp_s, rbp_r, rbm_s, rbm_r, rx_s, rx_r,
    h1_s, h1_r, hf_s, hf_r, hb_s, hb_r,
):
    s = lax.axis_index("section")
    r = lax.axis_index("row")
    c = lax.axis_index("col")
    z, xl = c // 2, c % 2
    xo = 1 - xl
    ns = lax.axis_size("section")
    sp, sm = (s + 1) % ns, (s + ns - 1) % ns
    up1, dn1 = (z + 1) % 8, (z + 7) % 8
    zp = {"col": up1 * 2 + xl}
    zm = {"col": dn1 * 2 + xl}
    xp = {"col": z * 2 + xo}
    mate = {"row": 1 - r}
    zp2 = {"col": ((z + 2) % 8) * 2 + xl}
    zm2 = {"col": ((z + 6) % 8) * 2 + xl}

    def at(sec, zz, x):
        return {"section": sec, "col": zz * 2 + x}

    def fetch(src, dst, i):
        cp = pltpu.make_async_copy(src, dst, lsem.at[i])
        cp.start()
        return cp

    cp_gate = fetch(gate_in.at[0], gv, 0)
    cp_f = fetch(in_f.at[0], gf.at[z, xl], 1)
    cp_b = fetch(in_b.at[0], gb.at[z, xl], 2)
    cp_dn = fetch(dn_in, dnv, 4)
    cp_up = fetch(up_in, upv, 3)

    barrier = pltpu.get_barrier_semaphore()
    for dev in (zp, zm, xp, mate):
        pl.semaphore_signal(barrier, inc=1, device_id=dev, device_id_type=MESH)

    @pl.when(z == 0)
    def _():
        for sec in (sp, sm):
            pl.semaphore_signal(barrier, inc=1, device_id={"section": sec}, device_id_type=MESH)
        pl.semaphore_wait(barrier, 6)

    @pl.when(z > 0)
    def _():
        pl.semaphore_wait(barrier, 4)

    sent = []

    def rc(src, dst, ss, rs, dev):
        return pltpu.make_async_remote_copy(
            src_ref=src, dst_ref=dst, send_sem=ss, recv_sem=rs, device_id=dev, device_id_type=MESH
        )

    def put(src, dst, ss, rs, dev):
        cp = rc(src, dst, ss, rs, dev)
        cp.start()
        sent.append(cp)

    def got(dst, rs):
        rc(dst, dst, rs, rs, zp).wait_recv()

    put(in_b.at[0], gb.at[z, xl], bx_s.at[0], bx_r.at[0], xp)
    put(in_f.at[0], gf.at[z, xl], fzp_s.at[0], fzp_r.at[0], zp)
    put(in_f.at[0], gf.at[z, xl], fzm_s.at[0], fzm_r.at[0], zm)
    put(in_b.at[0], gb.at[z, xl], bzp_s.at[0], bzp_r.at[0], zp)
    put(in_b.at[0], gb.at[z, xl], bzm_s.at[0], bzm_r.at[0], zm)
    put(in_f.at[0], gf.at[z, xl], fx_s.at[0], fx_r.at[0], xp)

    cp_gate.wait()
    g32 = gv[...].astype(F32)
    sg = 1.0 / (1.0 + jnp.exp(-g32))
    gs[...] = g32 * sg
    dg[...] = sg * (1.0 + g32 * (1.0 - sg))

    got(gb.at[z, xo], bx_r.at[0])
    put(gb.at[z, xo], gb.at[z, xo], bzp_s.at[3], bzp_r.at[3], zp)
    put(gb.at[z, xo], gb.at[z, xo], bzm_s.at[4], bzm_r.at[4], zm)
    for d in range(1, 5):
        lo, hi = (z + 8 - d) % 8, (z + d) % 8
        got(gf.at[lo, xl], fzp_r.at[d - 1])
        if d < 3:
            put(gf.at[lo, xl], gf.at[lo, xl], fzp_s.at[d], fzp_r.at[d], zp)
        if d == 2:
            put(gf.at[lo, xl], gf.at[lo, xl], fzp_s.at[3], fzp_r.at[3], zp2)
        put(gf.at[lo, xl], gf.at[lo, xl], fx_s.at[d], fx_r.at[d], xp)
        if d <= 3:
            got(gf.at[hi, xl], fzm_r.at[d - 1])
            if d < 3:
                put(gf.at[hi, xl], gf.at[hi, xl], fzm_s.at[d], fzm_r.at[d], zm)
            put(gf.at[hi, xl], gf.at[hi, xl], fx_s.at[4 + d], fx_r.at[4 + d], xp)
        for half, x in ((0, xl), (1, xo)):
            if d <= 3:
                i = half * 3 + d - 1
                got(gb.at[lo, x], bzp_r.at[i])
                if d < 3:
                    put(gb.at[lo, x], gb.at[lo, x], bzp_s.at[i + 1], bzp_r.at[i + 1], zp)
            i = half * 4 + d - 1
            got(gb.at[hi, x], bzm_r.at[i])
            if d < 3:
                put(gb.at[hi, x], gb.at[hi, x], bzm_s.at[i + 1], bzm_r.at[i + 1], zm)
            if d == 2:
                put(gb.at[hi, x], gb.at[hi, x], bzm_s.at[i + 2], bzm_r.at[i + 2], zm2)
    cp_b.wait()
    cp_dn.wait()
    grd = gb[...].reshape(128, 2048)
    for i, (a, w) in enumerate(CUTS):
        v = lax.dot_general(grd, dnv[a : a + w, :], NT, preferred_element_type=F32)
        hb[:, a : a + w] = v
        s1b[:, a : a + w] = v.astype(BF16)
        put(s1b.at[:, a : a + w], r1b.at[:, a : a + w], e_s.at[2 + i], e_r.at[2 + i], mate)

    got(gf.at[z, xo], fx_r.at[0])
    for d in range(1, 5):
        got(gf.at[(z + 8 - d) % 8, xo], fx_r.at[d])
        if d <= 3:
            got(gf.at[(z + d) % 8, xo], fx_r.at[4 + d])
    cp_f.wait()

    @pl.when(z == 0)
    def _():
        for sec in (sp, sm):
            pl.semaphore_signal(far, inc=1, device_id={"section": sec}, device_id_type=MESH)

    cp_up.wait()
    act = gf[...].reshape(128, 2048)
    for i, (a, w) in enumerate(CUTS):
        v = lax.dot_general(act, upv[:, a : a + w], NN, preferred_element_type=F32)
        uf[:, a : a + w] = v
        s1f[:, a : a + w] = v.astype(BF16)
        put(s1f.at[:, a : a + w], r1f.at[:, a : a + w], e_s.at[i], e_r.at[i], mate)

    chains = {
        (0, 0): (pb, sbp, rbp, rbp_s, rbp_r, B_LEN[0]),
        (0, 1): (pb, sbm, rbm, rbm_s, rbm_r, B_LEN[1]),
        (1, 0): (pf, sfp, rfp, rfp_s, rfp_r, F_LEN[0]),
        (1, 1): (pf, sfm, rfm, rfm_s, rfm_r, F_LEN[1]),
    }
    ends = {0: (mb, hb_s, hb_r, sm), 1: (mf, hf_s, hf_r, sp)}

    def chain(t, way, k):
        part, snd, rcv, ss, rs, n = chains[t, way]
        if k >= n:
            return
        d = n - k
        target = (z + d) % 8 if way == 0 else (z + 8 - d) % 8
        for j, x in enumerate((xl, xo)):
            v = part[target, x]
            if k > 0:
                got(rcv.at[k - 1, x], rs.at[2 * k - 2 + j])
                v = v + rcv[k - 1, x].astype(F32)
            snd[k, x] = v.astype(BF16)
            if d > 1:
                put(snd.at[k, x], rcv.at[k, x], ss.at[2 * k + j], rs.at[2 * k + j], zp if way == 0 else zm)
            else:
                land, fs, fr, sec = ends[t]
                i = way * 2 + j
                put(snd.at[k, x], land.at[i], fs.at[i], fr.at[i], at(sec, target, x))

    def share(t, part, snd, rcv):
        snd[...] = part[z, xo].astype(BF16)
        put(snd, rcv, rx_s.at[t], rx_r.at[t], xp)

    def hand(t, part, rcv, buf, m, n, sec):
        got(rcv, rx_r.at[t])
        m[...] = part[z, xl] + buf[z, xl].astype(F32) + rcv[...].astype(F32)
        put(m, n, h1_s.at[t], h1_r.at[t], at(sec, z, xl))

    for i, (a, w) in enumerate(CUTS):
        got(r1b.at[:, a : a + w], e_r.at[2 + i])
    h = hb[...] + r1b[...].astype(F32)
    hb[...] = h
    upg = (gs[...] * h).astype(BF16)
    for a in range(0, 2048, 512):
        v = lax.dot_general(upg, upv[a : a + 512, :], NT, preferred_element_type=F32)
        pb[:, :, :, a : a + 512] = v.reshape(8, 2, 8, 512)
    share(0, pb, sxb, rxb)
    chain(0, 0, 0)
    chain(0, 1, 0)

    for i, (a, w) in enumerate(CUTS):
        got(r1f.at[:, a : a + w], e_r.at[i])
    u = uf[...] + r1f[...].astype(F32)
    uf[...] = u
    hid = (gs[...] * u).astype(BF16)
    for a in range(0, 2048, 512):
        v = lax.dot_general(hid, dnv[:, a : a + 512], NN, preferred_element_type=F32)
        pf[:, :, :, a : a + 512] = v.reshape(8, 2, 8, 512)
    share(1, pf, sxf, rxf)
    chain(1, 1, 0)
    chain(1, 0, 0)

    chain(0, 0, 1)
    chain(0, 1, 1)

    @pl.when(z == 0)
    def _():
        pl.semaphore_wait(far, 2)
        for k in range(1, 8):
            pl.semaphore_signal(near, inc=1, device_id={"col": k * 2 + xl}, device_id_type=MESH)

    rows = pl.ds(pl.multiple_of(r * 64, 64), 64)
    out_g[0] = (hb[rows, :] * uf[rows, :] * dg[rows, :]).astype(BF16)
    chain(1, 1, 1)
    chain(1, 0, 1)

    @pl.when(z > 0)
    def _():
        pl.semaphore_wait(near, 1)

    chain(0, 0, 2)
    chain(0, 1, 2)
    hand(0, pb, rxb, gb, m1b, n1b, sm)
    chain(1, 1, 2)
    chain(1, 0, 2)
    hand(1, pf, rxf, gf, m1f, n1f, sp)
    chain(0, 0, 3)
    chain(1, 1, 3)

    for t, (n1, land, fr, out) in ((0, (n1b, mb, hb_r, out_b)), (1, (n1f, mf, hf_r, out_f))):
        got(n1, h1_r.at[t])
        v = n1[...]
        for i in (2, 3, 0, 1):
            got(land.at[i], fr.at[i])
            v = v + land[i].astype(F32)
        out[0] = v.astype(BF16)

    for cp in sent:
        cp.wait_send()


def writer(a, b, c, x, y, w, sem):
    stores = [pltpu.make_async_copy(p, q, sem.at[i]) for i, (p, q) in enumerate(((a, x), (b, y), (c, w)))]
    for cp in stores:
        cp.start()
    for cp in stores:
        cp.wait()


def shards(inputs, gate_pre, up_weight, down_weight, output_grad):
    vm = pltpu.VMEM
    dma = lambda n: [pltpu.SemaphoreType.DMA((n,)), pltpu.SemaphoreType.DMA((n,))]
    blk = lambda *n: vm((*n, 8, 2048), BF16)
    wide = lambda: vm((8, 2048), F32)
    mat = lambda t: vm((128, 896), t)
    any_spec = pl.BlockSpec(memory_space=pl.ANY)
    in_vmem = pl.BlockSpec(memory_space=pltpu.VMEM)
    shapes = (
        jax.ShapeDtypeStruct((1, 8, 2048), BF16),
        jax.ShapeDtypeStruct((1, 64, 896), BF16),
        jax.ShapeDtypeStruct((1, 8, 2048), BF16),
    )
    results = pl.pallas_call(
        kernel,
        out_shape=tuple(vm(x.shape, x.dtype) for x in shapes),
        in_specs=[any_spec] * 5,
        out_specs=(in_vmem,) * 3,
        scratch_shapes=[
            blk(8, 2), blk(8, 2), vm((2048, 896), BF16), vm((896, 2048), BF16), mat(BF16), mat(F32), mat(F32),
            mat(F32), mat(F32), mat(BF16), mat(BF16), mat(BF16), mat(BF16),
            vm((8, 2, 8, 2048), F32), vm((8, 2, 8, 2048), F32),
            blk(3, 2), blk(2, 2), blk(4, 2), blk(3, 2), blk(4, 2), blk(3, 2), blk(3, 2), blk(2, 2),
            blk(), blk(), blk(), blk(),
            wide(), wide(), wide(), wide(), blk(4), blk(4),
            pltpu.SemaphoreType.DMA((5,)), pltpu.SemaphoreType.REGULAR, pltpu.SemaphoreType.REGULAR,
            *dma(4), *dma(3), *dma(8), *dma(6), *dma(8), *dma(1),
            *dma(4), *dma(2 * F_LEN[0]), *dma(2 * F_LEN[1]), *dma(2 * B_LEN[0]), *dma(2 * B_LEN[1]), *dma(2),
            *dma(2), *dma(4), *dma(4),
        ],
        compiler_params=pltpu.CompilerParams(
            collective_id=0, has_side_effects=True, vmem_limit_bytes=60 * 1024 * 1024
        ),
        name="ffn",
    )(inputs, gate_pre, up_weight, down_weight, output_grad)
    return pl.pallas_call(
        writer,
        out_shape=shapes,
        in_specs=[in_vmem] * 3,
        out_specs=(any_spec,) * 3,
        scratch_shapes=[pltpu.SemaphoreType.DMA((3,))],
        name="write",
    )(*(pltpu.with_memory_space_constraint(x, pltpu.VMEM) for x in results))


def solution(mesh):
    placed = (
        P("section", "col", "row"),
        P("section", None, "col"),
        P("row", "col"),
        P("col", "row"),
        P("section", "col", "row"),
    )
    return jax.shard_map(
        shards,
        mesh=mesh,
        in_specs=placed,
        out_specs=(
            P("section", "col", "row"),
            P("section", "row", "col"),
            P("section", "col", "row"),
        ),
        check_vma=False,
    )
```

```python
import jax
import jax.numpy as jnp
from jax import lax
from jax.experimental import pallas as pl
from jax.experimental.pallas import tpu as pltpu
from jax.sharding import PartitionSpec as P

MESH = pl.DeviceIdType.MESH
F32 = jnp.float32
BF16 = jnp.bfloat16
NT = (((1,), (1,)), ((), ()))
NN = (((1,), (0,)), ((), ()))
CUTS = ((0, 512), (512, 384))
B_LEN = (4, 3)
F_LEN = (4, 3)


def kernel(
    in_f, gate_in, up_in, dn_in, in_b,
    out_f, out_g, out_b,
    gf, gb, upv, dnv, gv, gs, dg,
    uf, hb, s1f, r1f, s1b, r1b,
    pf, pb, sfp, rfp, sfm, rfm, sbp, rbp, sbm, rbm, sxf, rxf, sxb, rxb,
    m1f, n1f, m1b, n1b, mf, mb,
    lsem, near, far, fzp_s, fzp_r, fzm_s, fzm_r, fx_s, fx_r, bzp_s, bzp_r, bzm_s, bzm_r, bx_s, bx_r,
    e_s, e_r, rfp_s, rfp_r, rfm_s, rfm_r, rbp_s, rbp_r, rbm_s, rbm_r, rx_s, rx_r,
    h1_s, h1_r, hf_s, hf_r, hb_s, hb_r,
):
    s = lax.axis_index("section")
    r = lax.axis_index("row")
    c = lax.axis_index("col")
    z, xl = c // 2, c % 2
    xo = 1 - xl
    ns = lax.axis_size("section")
    sp, sm = (s + 1) % ns, (s + ns - 1) % ns
    up1, dn1 = (z + 1) % 8, (z + 7) % 8
    zp = {"col": up1 * 2 + xl}
    zm = {"col": dn1 * 2 + xl}
    xp = {"col": z * 2 + xo}
    mate = {"row": 1 - r}
    zp2 = {"col": ((z + 2) % 8) * 2 + xl}
    zm2 = {"col": ((z + 6) % 8) * 2 + xl}

    def at(sec, zz, x):
        return {"section": sec, "col": zz * 2 + x}

    def fetch(src, dst, i):
        cp = pltpu.make_async_copy(src, dst, lsem.at[i])
        cp.start()
        return cp

    cp_gate = fetch(gate_in.at[0], gv, 0)
    cp_f = fetch(in_f.at[0], gf.at[z, xl], 1)
    cp_b = fetch(in_b.at[0], gb.at[z, xl], 2)
    cp_dn = fetch(dn_in, dnv, 4)
    cp_up = fetch(up_in, upv, 3)

    barrier = pltpu.get_barrier_semaphore()
    for dev in (zp, zm, xp, mate):
        pl.semaphore_signal(barrier, inc=1, device_id=dev, device_id_type=MESH)

    @pl.when(z == 0)
    def _():
        for sec in (sp, sm):
            pl.semaphore_signal(barrier, inc=1, device_id={"section": sec}, device_id_type=MESH)
        pl.semaphore_wait(barrier, 6)

    @pl.when(z > 0)
    def _():
        pl.semaphore_wait(barrier, 4)

    sent = []

    def rc(src, dst, ss, rs, dev):
        return pltpu.make_async_remote_copy(
            src_ref=src, dst_ref=dst, send_sem=ss, recv_sem=rs, device_id=dev, device_id_type=MESH
        )

    def put(src, dst, ss, rs, dev):
        cp = rc(src, dst, ss, rs, dev)
        cp.start()
        sent.append(cp)

    def got(dst, rs):
        rc(dst, dst, rs, rs, zp).wait_recv()

    put(in_b.at[0], gb.at[z, xl], bx_s.at[0], bx_r.at[0], xp)
    put(in_f.at[0], gf.at[z, xl], fzp_s.at[0], fzp_r.at[0], zp)
    put(in_f.at[0], gf.at[z, xl], fzm_s.at[0], fzm_r.at[0], zm)
    put(in_b.at[0], gb.at[z, xl], bzp_s.at[0], bzp_r.at[0], zp)
    put(in_b.at[0], gb.at[z, xl], bzm_s.at[0], bzm_r.at[0], zm)
    put(in_f.at[0], gf.at[z, xl], fx_s.at[0], fx_r.at[0], xp)

    cp_gate.wait()
    g32 = gv[...].astype(F32)
    sg = 1.0 / (1.0 + jnp.exp(-g32))
    gs[...] = g32 * sg
    dg[...] = sg * (1.0 + g32 * (1.0 - sg))

    got(gb.at[z, xo], bx_r.at[0])
    put(gb.at[z, xo], gb.at[z, xo], bzp_s.at[3], bzp_r.at[3], zp)
    put(gb.at[z, xo], gb.at[z, xo], bzm_s.at[4], bzm_r.at[4], zm)
    for d in range(1, 5):
        lo, hi = (z + 8 - d) % 8, (z + d) % 8
        got(gf.at[lo, xl], fzp_r.at[d - 1])
        if d < 3:
            put(gf.at[lo, xl], gf.at[lo, xl], fzp_s.at[d], fzp_r.at[d], zp)
        if d == 2:
            put(gf.at[lo, xl], gf.at[lo, xl], fzp_s.at[3], fzp_r.at[3], zp2)
        put(gf.at[lo, xl], gf.at[lo, xl], fx_s.at[d], fx_r.at[d], xp)
        if d <= 3:
            got(gf.at[hi, xl], fzm_r.at[d - 1])
            if d < 3:
                put(gf.at[hi, xl], gf.at[hi, xl], fzm_s.at[d], fzm_r.at[d], zm)
            put(gf.at[hi, xl], gf.at[hi, xl], fx_s.at[4 + d], fx_r.at[4 + d], xp)
        for half, x in ((0, xl), (1, xo)):
            if d <= 3:
                i = half * 3 + d - 1
                got(gb.at[lo, x], bzp_r.at[i])
                if d < 3:
                    put(gb.at[lo, x], gb.at[lo, x], bzp_s.at[i + 1], bzp_r.at[i + 1], zp)
            i = half * 4 + d - 1
            got(gb.at[hi, x], bzm_r.at[i])
            if d < 3:
                put(gb.at[hi, x], gb.at[hi, x], bzm_s.at[i + 1], bzm_r.at[i + 1], zm)
            if d == 2:
                put(gb.at[hi, x], gb.at[hi, x], bzm_s.at[i + 2], bzm_r.at[i + 2], zm2)
    cp_b.wait()
    cp_dn.wait()
    grd = gb[...].reshape(128, 2048)
    for i, (a, w) in enumerate(CUTS):
        v = lax.dot_general(grd, dnv[a : a + w, :], NT, preferred_element_type=F32)
        hb[:, a : a + w] = v
        s1b[:, a : a + w] = v.astype(BF16)
        put(s1b.at[:, a : a + w], r1b.at[:, a : a + w], e_s.at[2 + i], e_r.at[2 + i], mate)

    got(gf.at[z, xo], fx_r.at[0])
    for d in range(1, 5):
        got(gf.at[(z + 8 - d) % 8, xo], fx_r.at[d])
        if d <= 3:
            got(gf.at[(z + d) % 8, xo], fx_r.at[4 + d])
    cp_f.wait()

    @pl.when(z == 0)
    def _():
        for sec in (sp, sm):
            pl.semaphore_signal(far, inc=1, device_id={"section": sec}, device_id_type=MESH)

    cp_up.wait()
    act = gf[...].reshape(128, 2048)
    for i, (a, w) in enumerate(CUTS):
        v = lax.dot_general(act, upv[:, a : a + w], NN, preferred_element_type=F32)
        uf[:, a : a + w] = v
        s1f[:, a : a + w] = v.astype(BF16)
        put(s1f.at[:, a : a + w], r1f.at[:, a : a + w], e_s.at[i], e_r.at[i], mate)

    chains = {
        (0, 0): (pb, sbp, rbp, rbp_s, rbp_r, B_LEN[0]),
        (0, 1): (pb, sbm, rbm, rbm_s, rbm_r, B_LEN[1]),
        (1, 0): (pf, sfp, rfp, rfp_s, rfp_r, F_LEN[0]),
        (1, 1): (pf, sfm, rfm, rfm_s, rfm_r, F_LEN[1]),
    }
    ends = {0: (mb, hb_s, hb_r, sm), 1: (mf, hf_s, hf_r, sp)}

    def chain(t, way, k):
        part, snd, rcv, ss, rs, n = chains[t, way]
        if k >= n:
            return
        d = n - k
        target = (z + d) % 8 if way == 0 else (z + 8 - d) % 8
        for j, x in enumerate((xl, xo)):
            v = part[target, x]
            if k > 0:
                got(rcv.at[k - 1, x], rs.at[2 * k - 2 + j])
                v = v + rcv[k - 1, x].astype(F32)
            snd[k, x] = v.astype(BF16)
            if d > 1:
                put(snd.at[k, x], rcv.at[k, x], ss.at[2 * k + j], rs.at[2 * k + j], zp if way == 0 else zm)
            else:
                land, fs, fr, sec = ends[t]
                i = way * 2 + j
                put(snd.at[k, x], land.at[i], fs.at[i], fr.at[i], at(sec, target, x))

    def share(t, part, snd, rcv):
        snd[...] = part[z, xo].astype(BF16)
        put(snd, rcv, rx_s.at[t], rx_r.at[t], xp)

    def hand(t, part, rcv, buf, m, n, sec):
        got(rcv, rx_r.at[t])
        m[...] = part[z, xl] + buf[z, xl].astype(F32) + rcv[...].astype(F32)
        put(m, n, h1_s.at[t], h1_r.at[t], at(sec, z, xl))

    for i, (a, w) in enumerate(CUTS):
        got(r1b.at[:, a : a + w], e_r.at[2 + i])
    h = hb[...] + r1b[...].astype(F32)
    hb[...] = h
    upg = (gs[...] * h).astype(BF16)
    for a in range(0, 2048, 512):
        v = lax.dot_general(upg, upv[a : a + 512, :], NT, preferred_element_type=F32)
        pb[:, :, :, a : a + 512] = v.reshape(8, 2, 8, 512)
    share(0, pb, sxb, rxb)
    chain(0, 0, 0)
    chain(0, 1, 0)

    for i, (a, w) in enumerate(CUTS):
        got(r1f.at[:, a : a + w], e_r.at[i])
    u = uf[...] + r1f[...].astype(F32)
    uf[...] = u
    hid = (gs[...] * u).astype(BF16)
    for a in range(0, 2048, 512):
        v = lax.dot_general(hid, dnv[:, a : a + 512], NN, preferred_element_type=F32)
        pf[:, :, :, a : a + 512] = v.reshape(8, 2, 8, 512)
    share(1, pf, sxf, rxf)
    chain(1, 0, 0)
    chain(1, 1, 0)

    chain(0, 0, 1)
    chain(0, 1, 1)

    @pl.when(z == 0)
    def _():
        pl.semaphore_wait(far, 2)
        for k in range(1, 8):
            pl.semaphore_signal(near, inc=1, device_id={"col": k * 2 + xl}, device_id_type=MESH)

    rows = pl.ds(pl.multiple_of(r * 64, 64), 64)
    out_g[0] = (hb[rows, :] * uf[rows, :] * dg[rows, :]).astype(BF16)
    chain(1, 0, 1)
    chain(1, 1, 1)

    @pl.when(z > 0)
    def _():
        pl.semaphore_wait(near, 1)

    chain(0, 0, 2)
    chain(0, 1, 2)
    hand(0, pb, rxb, gb, m1b, n1b, sm)
    chain(1, 0, 2)
    chain(1, 1, 2)
    hand(1, pf, rxf, gf, m1f, n1f, sp)
    chain(0, 0, 3)
    chain(1, 0, 3)

    for t, (n1, land, fr, out) in ((0, (n1b, mb, hb_r, out_b)), (1, (n1f, mf, hf_r, out_f))):
        got(n1, h1_r.at[t])
        v = n1[...]
        for i in (2, 3, 0, 1):
            got(land.at[i], fr.at[i])
            v = v + land[i].astype(F32)
        out[0] = v.astype(BF16)

    for cp in sent:
        cp.wait_send()


def writer(a, b, c, x, y, w, sem):
    stores = [pltpu.make_async_copy(p, q, sem.at[i]) for i, (p, q) in enumerate(((a, x), (b, y), (c, w)))]
    for cp in stores:
        cp.start()
    for cp in stores:
        cp.wait()


def shards(inputs, gate_pre, up_weight, down_weight, output_grad):
    vm = pltpu.VMEM
    dma = lambda n: [pltpu.SemaphoreType.DMA((n,)), pltpu.SemaphoreType.DMA((n,))]
    blk = lambda *n: vm((*n, 8, 2048), BF16)
    wide = lambda: vm((8, 2048), F32)
    mat = lambda t: vm((128, 896), t)
    any_spec = pl.BlockSpec(memory_space=pl.ANY)
    in_vmem = pl.BlockSpec(memory_space=pltpu.VMEM)
    shapes = (
        jax.ShapeDtypeStruct((1, 8, 2048), BF16),
        jax.ShapeDtypeStruct((1, 64, 896), BF16),
        jax.ShapeDtypeStruct((1, 8, 2048), BF16),
    )
    results = pl.pallas_call(
        kernel,
        out_shape=tuple(vm(x.shape, x.dtype) for x in shapes),
        in_specs=[any_spec] * 5,
        out_specs=(in_vmem,) * 3,
        scratch_shapes=[
            blk(8, 2), blk(8, 2), vm((2048, 896), BF16), vm((896, 2048), BF16), mat(BF16), mat(F32), mat(F32),
            mat(F32), mat(F32), mat(BF16), mat(BF16), mat(BF16), mat(BF16),
            vm((8, 2, 8, 2048), F32), vm((8, 2, 8, 2048), F32),
            blk(4, 2), blk(3, 2), blk(3, 2), blk(2, 2), blk(4, 2), blk(3, 2), blk(3, 2), blk(2, 2),
            blk(), blk(), blk(), blk(),
            wide(), wide(), wide(), wide(), blk(4), blk(4),
            pltpu.SemaphoreType.DMA((5,)), pltpu.SemaphoreType.REGULAR, pltpu.SemaphoreType.REGULAR,
            *dma(4), *dma(3), *dma(8), *dma(6), *dma(8), *dma(1),
            *dma(4), *dma(2 * F_LEN[0]), *dma(2 * F_LEN[1]), *dma(2 * B_LEN[0]), *dma(2 * B_LEN[1]), *dma(2),
            *dma(2), *dma(4), *dma(4),
        ],
        compiler_params=pltpu.CompilerParams(
            collective_id=0, has_side_effects=True, vmem_limit_bytes=60 * 1024 * 1024
        ),
        name="ffn",
    )(inputs, gate_pre, up_weight, down_weight, output_grad)
    return pl.pallas_call(
        writer,
        out_shape=shapes,
        in_specs=[in_vmem] * 3,
        out_specs=(any_spec,) * 3,
        scratch_shapes=[pltpu.SemaphoreType.DMA((3,))],
        name="write",
    )(*(pltpu.with_memory_space_constraint(x, pltpu.VMEM) for x in results))


def solution(mesh):
    placed = (
        P("section", "col", "row"),
        P("section", None, "col"),
        P("row", "col"),
        P("col", "row"),
        P("section", "col", "row"),
    )
    return jax.shard_map(
        shards,
        mesh=mesh,
        in_specs=placed,
        out_specs=(
            P("section", "col", "row"),
            P("section", "row", "col"),
            P("section", "col", "row"),
        ),
        check_vma=False,
    )
```
